256 devices in a mesh: snap: 16 (over z, core), vert: 16 (over y, x).
Axes of the slice: x: 4, y: 4, z: 8, core: 2. Of those that a mesh axis runs over, the one named last changes fastest.
Arguments:
- saved_gates: bfloat16 [16, 8192, 1536], P(None, ('vert', 'snap')), may hold values from -1 to 1, as said below
- saved_cells: bfloat16 [16, 8192, 384], P(None, ('vert', 'snap')), may hold values from -4 to 4
- conv_out: float32 [16, 8192, 384], P(None, ('vert', 'snap')), may hold values from -6 to 6
- out_grad: float32 [16, 8192, 384], P(None, ('vert', 'snap')), may hold values from -6 to 6
- input_weight: float32 [384, 1536], replicated, may hold values from -0.3125 to 0.3125
- recur_weight: float32 [384, 1536], replicated, may hold values from -0.3125 to 0.3125
- conv_weight: float32 [384, 384], replicated, may hold values from -0.3125 to 0.3125
- node_feats: float32 [16, 8192, 384], P('snap', 'vert'), may hold values from -6 to 6
- tile_values: bfloat16 [16, 16, 5, 512, 512], P('snap', 'vert'), may hold values from -0.15625 to 0.15625
- tile_mask: int32 [16, 16, 5], P('snap', 'vert'), may hold values 0 or 1
Outputs:
- feat_grad: float32 [16, 8192, 384], P('snap', 'vert')
- conv_weight_grad: float32 [147456], P(('snap', 'vert'))
- input_weight_grad: float32 [589824], P(('snap', 'vert'))
- recur_weight_grad: float32 [589824], P(('snap', 'vert'))
The draws below stay inside these ranges and needn't reach their ends.
Inputs may be any that keep to these rules, and one draw needn't show every extreme that they name: `saved_gates`: the first and fourth blocks of 384 entries lie strictly between 0 and 1, the second in (0, 1], the third strictly between -1 and 1.
All inputs are finite; a program needn't handle non-finite values. No bound on the sum of `tile_mask` on one device may be relied on, other than what follows from the above.
Results may differ from the reference program's by a relative error of at most 0.0029.
Values may be sent and summed in bfloat16 or wider, within the bound.
A program may use at most 128 MiB of HBM per device.

```python
import math
import jax
import jax.numpy as jnp
from jax import lax

F = 384
G = 1536
BLOCK = 512
REACH = 2
SLOTS = 5
SNAPS = 16
VERTS = 8192
N_VERT = 16


def draw_saved_gates(key, part):
    keys = jax.random.split(key, 5)
    shape = (SNAPS, VERTS, F)
    in_gate = jax.random.uniform(keys[0], shape, jnp.float32, 0.05, 0.95)
    out_gate = jax.random.uniform(keys[1], shape, jnp.float32, 0.05, 0.95)
    rates = jnp.exp(jax.random.uniform(keys[2], (F,), jnp.float32, math.log(0.005), math.log(1.0)))
    jitter = jax.random.uniform(keys[3], shape, jnp.float32, 0.5, 1.5)
    forget = jnp.exp(-rates[None, None, :] * jitter)
    candidate = jax.random.uniform(keys[4], shape, jnp.float32, -0.95, 0.95)
    joined = jnp.concatenate([in_gate, forget, candidate, out_gate], axis=-1)
    return joined.astype(jnp.bfloat16)


def plant(entries, stream_key, smallest, high):
    dims = entries.shape
    index_at = [jax.random.randint(jax.random.fold_in(stream_key, axis), (), 0, dims[axis]) for axis in range(len(dims))]
    entries = entries.at[tuple(index_at)].set(smallest)
    longest = dims.index(max(dims))
    index_at[longest] = (index_at[longest] + 1) % dims[longest]
    return entries.at[tuple(index_at)].set(high)


def block_levels(stream_key, dims, cuts, least, top_value):
    loudness, own = 1.0, jax.random.fold_in(stream_key, 6)
    for axis_at, shards_of in cuts:
        steps = jnp.exp(jax.random.uniform(jax.random.fold_in(own, axis_at), (shards_of,), jnp.float32, least / len(cuts), top_value / len(cuts)))
        loudness = loudness * jnp.repeat(steps, dims[axis_at] // shards_of).reshape([-1 if axis == axis_at else 1 for axis in range(len(dims))])
    return loudness


def scatter_about(stream_key, extent, deviation, limit, pieces=(), held_as=jnp.bfloat16):
    loudness = block_levels(stream_key, extent, pieces, -0.22, 0.18) if pieces else 1.0
    result = jax.random.normal(stream_key, extent, jnp.float32) * deviation * loudness
    return jnp.minimum(jnp.maximum(result, -limit), limit).astype(held_as)


def setup_inputs(seed: int = 0) -> dict:
    key_of = jax.random.split(jax.random.key(seed), 11)
    return {
        "saved_gates": draw_saved_gates(jax.random.fold_in(key_of[10], 71), 0),
        "saved_cells": scatter_about(key_of[1], (SNAPS, VERTS, F), 1.0, 4.0, ((1, 256),)),
        "conv_out": scatter_about(key_of[2], (SNAPS, VERTS, F), 1.0, 6.0, ((1, 256),), jnp.float32),
        "out_grad": scatter_about(key_of[3], (SNAPS, VERTS, F), 1.0, 6.0, ((1, 256),), jnp.float32),
        "input_weight": scatter_about(key_of[4], (F, G), F ** -0.5, 0.3125, (), jnp.float32),
        "recur_weight": scatter_about(key_of[5], (F, G), F ** -0.5, 0.3125, (), jnp.float32),
        "conv_weight": scatter_about(key_of[6], (F, F), F ** -0.5, 0.3125, (), jnp.float32),
        "node_feats": scatter_about(key_of[7], (SNAPS, VERTS, F), 1.0, 6.0, ((0, 16), (1, 16)), jnp.float32),
        "tile_values": scatter_about(key_of[8], (SNAPS, N_VERT, SLOTS, BLOCK, BLOCK), (3 * BLOCK) ** -0.5, 0.15625, ((0, 16), (1, 16))),
        "tile_mask": plant((jax.random.randint(key_of[9], (SNAPS, N_VERT, SLOTS), 0, 3) < 2).astype(jnp.int32), jax.random.fold_in(key_of[9], 1), 0, 1),
    }


def cell_backward(saved_gates, saved_cells, out_grad, recur_weight):
    feat_width = saved_cells.shape[-1]
    gate_vals = saved_gates.astype(jnp.float32)
    cell_vals = saved_cells.astype(jnp.float32)
    prev_cells = jnp.concatenate([jnp.zeros_like(cell_vals[:1]), cell_vals[:-1]], axis=0)

    def reverse_step(carry, inputs):
        rec_grad, cell_grad = carry
        gate_now, cell_now, cell_before, grad_now = inputs
        in_gate = gate_now[:, :feat_width]
        forget = gate_now[:, feat_width:2 * feat_width]
        candidate = gate_now[:, 2 * feat_width:3 * feat_width]
        out_gate = gate_now[:, 3 * feat_width:]
        total_grad = grad_now + rec_grad
        squashed = jnp.tanh(cell_now)
        cell_total = cell_grad + total_grad * out_gate * (1.0 - squashed * squashed)
        pre_grad = jnp.concatenate([
            cell_total * candidate * in_gate * (1.0 - in_gate),
            cell_total * cell_before * forget * (1.0 - forget),
            cell_total * in_gate * (1.0 - candidate * candidate),
            total_grad * squashed * out_gate * (1.0 - out_gate)], axis=-1)
        new_rec = jnp.dot(pre_grad, recur_weight.T, precision=lax.Precision.HIGHEST, preferred_element_type=jnp.float32)
        return (new_rec, cell_total * forget), pre_grad

    row_total = cell_vals.shape[1]
    begin = (jnp.zeros((row_total, feat_width), jnp.float32), jnp.zeros((row_total, feat_width), jnp.float32))
    unused, pre_grads = lax.scan(reverse_step, begin, (gate_vals, cell_vals, prev_cells, out_grad), reverse=True)
    last_out = gate_vals[:, :, 3 * feat_width:]
    prev_out = jnp.concatenate([jnp.zeros_like(last_out[:1]), last_out[:-1]], axis=0)
    prev_hidden = prev_out * jnp.tanh(prev_cells)
    return pre_grads, prev_hidden


def reference(saved_gates, saved_cells, conv_out, out_grad, input_weight, recur_weight, conv_weight, node_feats, tile_values, tile_mask):
    pre_grads, prev_hidden = cell_backward(saved_gates, saved_cells, out_grad, recur_weight)
    conv_in_grad = jnp.einsum('tvg,fg->tvf', pre_grads, input_weight, precision=lax.Precision.HIGHEST)
    input_weight_grad = jnp.einsum('tvf,tvg->fg', conv_out, pre_grads, precision=lax.Precision.HIGHEST).reshape(-1)
    recur_weight_grad = jnp.einsum('tvf,tvg->fg', prev_hidden, pre_grads, precision=lax.Precision.HIGHEST).reshape(-1)

    def snapshot(inputs):
        tiles, mask_now, grad_h, feats = inputs
        rounded = lax.optimization_barrier(grad_h.astype(jnp.bfloat16)).astype(jnp.float32)
        blocks = rounded.reshape(N_VERT, BLOCK, F)
        partial_value = jnp.einsum('rkij,rif->rkjf', tiles.astype(jnp.float32), blocks, precision=lax.Precision.HIGHEST)
        offsets = jnp.arange(SLOTS, dtype=jnp.int32) - REACH
        target = jnp.arange(N_VERT, dtype=jnp.int32)[:, None] + offsets[None, :]
        present = (mask_now == 1) & (target >= 0) & (target < N_VERT)
        partial_value = partial_value * present.astype(jnp.float32)[:, :, None, None]
        z_grad = jnp.zeros((N_VERT, BLOCK, F), jnp.float32)
        for slot in range(SLOTS):
            offset = slot - REACH
            moved = partial_value[:, slot]
            if offset > 0:
                moved = jnp.concatenate([jnp.zeros((offset, BLOCK, F), jnp.float32), moved[:-offset]], axis=0)
            elif offset < 0:
                moved = jnp.concatenate([moved[-offset:], jnp.zeros((-offset, BLOCK, F), jnp.float32)], axis=0)
            z_grad = z_grad + moved
        z_grad = z_grad.reshape(VERTS, F)
        feat_now = jnp.dot(z_grad, conv_weight.T, precision=lax.Precision.HIGHEST, preferred_element_type=jnp.float32)
        term = jnp.dot(feats.T, z_grad, precision=lax.Precision.HIGHEST, preferred_element_type=jnp.float32)
        return feat_now, term

    feat_grad, terms = lax.map(snapshot, (tile_values, tile_mask, conv_in_grad, node_feats))
    conv_weight_grad = jnp.sum(terms, axis=0).reshape(-1)
    return feat_grad, conv_weight_grad, input_weight_grad, recur_weight_grad
```

```python
import jax
import jax.numpy as jnp
from jax import lax
from jax.experimental import pallas as pl
from jax.experimental.pallas import tpu as pltpu
from jax.sharding import PartitionSpec as P

F32, BF16 = jnp.float32, jnp.bfloat16
VMEM_CAP = 60 * 1024 * 1024


def split_store(value, hi_ref, lo_ref):
    high = value.astype(BF16)
    hi_ref[...] = high
    lo_ref[...] = (value - high.astype(F32)).astype(BF16)


def dot3(a_hi, a_lo, b_hi, b_lo, dims):
    one = lambda a, b: lax.dot_general(a, b, (dims, ((), ())), preferred_element_type=F32)
    return one(a_hi, b_hi) + (one(a_lo, b_hi) + one(a_hi, b_lo))


def scan_kernel(
    gates, cells, grads, recur_t, input_t,
    rounded, pre_hi, pre_lo, hid_hi, hid_lo,
    r_hi, r_lo, i_hi, i_lo, rec, cell_grad,
):
    steps, rows, feat = cells.shape
    split_store(recur_t[...], r_hi, r_lo)
    split_store(input_t[...], i_hi, i_lo)
    rec[...] = jnp.zeros_like(rec)
    cell_grad[...] = jnp.zeros_like(cell_grad)
    two = ((1,), (0,))

    def step(n, carry):
        t = steps - 1 - n
        before = jnp.maximum(t - 1, 0)
        live = (t > 0).astype(F32)
        part = lambda k: gates[t, :, k * feat : (k + 1) * feat].astype(F32)
        in_gate, forget, candidate, out_gate = part(0), part(1), part(2), part(3)
        squashed = jnp.tanh(cells[t].astype(F32))
        cell_before = cells[before].astype(F32) * live
        hidden = gates[before, :, 3 * feat :].astype(F32) * jnp.tanh(cell_before)
        high = hidden.astype(BF16)
        hid_hi[t] = high
        hid_lo[t] = (hidden - high.astype(F32)).astype(BF16)
        total = grads[t] + rec[...]
        cell_total = cell_grad[...] + total * (out_gate * (1.0 - squashed * squashed))
        pieces = [
            cell_total * (candidate * in_gate * (1.0 - in_gate)),
            cell_total * (cell_before * forget * (1.0 - forget)),
            cell_total * (in_gate * (1.0 - candidate * candidate)),
            total * (squashed * out_gate * (1.0 - out_gate)),
        ]
        cell_grad[...] = cell_total * forget
        acc = None
        for k, piece in enumerate(pieces):
            cols = slice(k * feat, (k + 1) * feat)
            high = piece.astype(BF16)
            low = (piece - high.astype(F32)).astype(BF16)
            pre_hi[t, :, cols] = high
            pre_lo[t, :, cols] = low
            both = jnp.concatenate([high, low], axis=0)
            main = jnp.dot(both, r_hi[cols, :], preferred_element_type=F32)
            side = jnp.dot(high, r_lo[cols, :], preferred_element_type=F32)
            term = main[:rows] + (main[rows:] + side)
            acc = term if acc is None else acc + term
        rec[...] = acc
        return carry

    lax.fori_loop(0, steps, step, 0)
    group = 4

    def project(n, carry):
        at = pl.ds(n * group, group)
        shape = (group * rows, 4 * feat)
        value = dot3(
            pre_hi[at].reshape(shape), pre_lo[at].reshape(shape), i_hi[...], i_lo[...], two
        )
        rounded[at] = value.astype(BF16).reshape(group, rows, feat)
        return carry

    lax.fori_loop(0, steps // group, project, 0)


def run_scan(gates, cells, grads, recur_t, input_t):
    steps, rows, feat = cells.shape
    wide = 4 * feat
    vm = pl.BlockSpec(memory_space=pltpu.VMEM)
    shape = lambda *s: jax.ShapeDtypeStruct(s, BF16)
    return pl.pallas_call(
        scan_kernel,
        in_specs=[vm] * 5,
        out_specs=[vm] * 5,
        out_shape=[
            shape(steps, rows, feat), shape(steps, rows, wide), shape(steps, rows, wide),
            shape(steps, rows, feat), shape(steps, rows, feat),
        ],
        scratch_shapes=[
            pltpu.VMEM((wide, feat), BF16), pltpu.VMEM((wide, feat), BF16),
            pltpu.VMEM((wide, feat), BF16), pltpu.VMEM((wide, feat), BF16),
            pltpu.VMEM((rows, feat), F32), pltpu.VMEM((rows, feat), F32),
        ],
        compiler_params=pltpu.CompilerParams(vmem_limit_bytes=VMEM_CAP),
        name="scan",
    )(gates, cells, grads, recur_t, input_t)


def weight_kernel(conv_out, hid_hi, hid_lo, pre_hi, pre_lo, out, c_hi, c_lo):
    rows, feat = conv_out.shape
    wide = pre_hi.shape[1]
    split_store(conv_out[...], c_hi, c_lo)
    first = ((0,), (0,))
    width = 512

    def block(n, carry):
        at = pl.ds(pl.multiple_of(n * width, width), width)
        p_hi, p_lo = pre_hi[:, at], pre_lo[:, at]
        out[0, :, at] = dot3(c_hi[...], c_lo[...], p_hi, p_lo, first).astype(out.dtype)
        out[1, :, at] = dot3(hid_hi[...], hid_lo[...], p_hi, p_lo, first).astype(out.dtype)
        return carry

    lax.fori_loop(0, wide // width, block, 0)


def run_weights(conv_out, hid_hi, hid_lo, pre_hi, pre_lo):
    rows, feat = conv_out.shape
    wide = pre_hi.shape[1]
    vm = pl.BlockSpec(memory_space=pltpu.VMEM)
    flops = 12 * rows * feat * wide
    return pl.pallas_call(
        weight_kernel,
        in_specs=[vm] * 5,
        out_specs=vm,
        out_shape=jax.ShapeDtypeStruct((2, feat, wide), BF16),
        scratch_shapes=[pltpu.VMEM((rows, feat), BF16), pltpu.VMEM((rows, feat), BF16)],
        compiler_params=pltpu.CompilerParams(vmem_limit_bytes=VMEM_CAP),
        cost_estimate=pl.CostEstimate(flops=flops, bytes_accessed=8 << 20, transcendentals=0),
        name="weights",
    )(conv_out, hid_hi, hid_lo, pre_hi, pre_lo)


def tile_kernel(present, tiles, rounded, away, home):
    slots = tiles.shape[0]
    reach = slots // 2
    at = 0
    for slot in range(slots):
        keep = present[slot].astype(F32)
        value = lax.dot_general(
            tiles[slot], rounded[...], (((0,), (0,)), ((), ())), preferred_element_type=F32
        ) * keep
        if slot == reach:
            home[...] = value
        else:
            away[at] = value.astype(BF16)
            at += 1


def run_tiles(present, tiles, rounded):
    slots, block, _ = tiles.shape
    feat = rounded.shape[1]
    vm = pl.BlockSpec(memory_space=pltpu.VMEM)
    return pl.pallas_call(
        tile_kernel,
        in_specs=[pl.BlockSpec(memory_space=pltpu.SMEM), vm, vm],
        out_specs=[vm, vm],
        out_shape=[
            jax.ShapeDtypeStruct((slots - 1, block, feat), BF16),
            jax.ShapeDtypeStruct((block, feat), F32),
        ],
        compiler_params=pltpu.CompilerParams(vmem_limit_bytes=VMEM_CAP),
        name="tiles",
    )(present, tiles, rounded)


def passed_along(shard, axis, by):
    size = lax.axis_size(axis)
    pairs = [(i, i + by) for i in range(size) if 0 <= i + by < size]
    return lax.ppermute(shard, axis, pairs)


def summed_pieces(pieces, axis):
    got = lax.all_to_all(pieces, axis, split_axis=0, concat_axis=0, tiled=True)
    return jnp.sum(got.astype(F32), axis=0)


def local(
    saved_gates, saved_cells, conv_out, out_grad, input_weight, recur_weight,
    conv_weight, node_feats, tile_values, tile_mask,
):
    steps, rows, feat = saved_cells.shape
    wide = 4 * feat
    snaps, blocks = lax.axis_size("snap"), lax.axis_size("vert")
    rounded, pre_hi, pre_lo, hid_hi, hid_lo = run_scan(
        saved_gates, saved_cells, out_grad, recur_weight.T, input_weight.T
    )
    arrived = lax.all_to_all(rounded, "snap", split_axis=0, concat_axis=1, tiled=True)
    flat = lambda a: a.reshape(steps * rows, a.shape[-1])
    terms = run_weights(flat(conv_out), flat(hid_hi), flat(hid_lo), flat(pre_hi), flat(pre_lo))
    own = feat // snaps
    terms = terms.reshape(2, snaps, own, wide).transpose(1, 0, 2, 3)

    tiles = tile_values[0, 0]
    slot_count = tiles.shape[0]
    reach = slot_count // 2
    target = lax.axis_index("vert") + jnp.arange(slot_count, dtype=jnp.int32) - reach
    inside = (target >= 0) & (target < blocks)
    present = ((tile_mask[0, 0] == 1) & inside).astype(jnp.int32)
    away, z_grad = run_tiles(present, tiles, arrived[0])
    offsets = [k - reach for k in range(slot_count) if k != reach]
    moved = [passed_along(away[n], "vert", by) for n, by in enumerate(offsets)]
    for part in moved:
        z_grad = z_grad + part.astype(F32)
    feat_grad = jnp.einsum(
        "bg,fg->bf", z_grad, conv_weight, precision=lax.Precision.HIGH, preferred_element_type=F32
    )[None]
    conv_term = jnp.einsum(
        "bf,bg->fg", node_feats[0], z_grad, precision=lax.Precision.HIGH, preferred_element_type=F32
    )
    first = summed_pieces(terms, "snap")
    lstm = first.reshape(2, blocks, own * wide // blocks).transpose(1, 0, 2)
    lstm = summed_pieces(lstm, "vert")
    conv = summed_pieces(conv_term.reshape(snaps, own, feat).astype(BF16), "snap")
    conv = summed_pieces(conv.reshape(blocks, own * feat // blocks), "vert")
    return (feat_grad, conv, lstm[0], lstm[1])


def solution(mesh):
    along = P(None, ("vert", "snap"), None)
    placed = (
        along, along, along, along, P(), P(), P(),
        P("snap", "vert", None), P("snap", "vert", None, None, None), P("snap", "vert", None),
    )
    both = P(("snap", "vert"))
    return jax.shard_map(
        local,
        mesh=mesh,
        in_specs=placed,
        out_specs=(P("snap", "vert", None), both, both, both),
        check_vma=False,
    )
```

```python
import jax
import jax.numpy as jnp
from jax import lax
from jax.experimental import pallas as pl
from jax.experimental.pallas import tpu as pltpu
from jax.sharding import PartitionSpec as P

F32, BF16 = jnp.float32, jnp.bfloat16
VMEM_CAP = 62 * 1024 * 1024
COL_BLOCKS = 3
GROUP = 4
MESH = pl.DeviceIdType.MESH


def halves(value):
    high = value.astype(BF16)
    return high, (value - high.astype(F32)).astype(BF16)


def split_store(value, hi_ref, lo_ref):
    hi_ref[...], lo_ref[...] = halves(value)


def dot3(a_hi, a_lo, b_hi, b_lo, dims):
    one = lambda a, b: lax.dot_general(a, b, (dims, ((), ())), preferred_element_type=F32)
    return one(a_hi, b_hi) + (one(a_lo, b_hi) + one(a_hi, b_lo))


def remote(src, dst, send, recv, device):
    return pltpu.make_async_remote_copy(
        src_ref=src, dst_ref=dst, send_sem=send, recv_sem=recv, device_id=device, device_id_type=MESH
    )


def whole_kernel(
    present, gates, cells, grads, recur, input_any, conv_out_any, tiles_any, feats_any, conv_w_any,
    feat_out, conv_out_sum, lstm_sum,
    input_w, conv_out, tiles, feats, conv_w,
    r_hi, r_lo, i_hi, i_lo, rec, cell_grad,
    pre_hi, pre_lo, hid_hi, hid_lo, c_hi, c_lo, rounded, arrived,
    terms, pair_out, pair_in, z_out, z_in, full, x_out, x_in,
    away, got, z_grad, z_hi, z_lo, w_hi, w_lo, n_hi, n_lo,
    ct, cp_out, cp_in, cz_out, cz_in, cx_out, cx_in,
    load_sem, a_send, a_recv, p_send, p_recv, z_send, z_recv, x_send, x_recv,
    t_send, t_recv, cp_send, cp_recv, cz_send, cz_recv, cx_send, cx_recv,
):
    steps, rows, feat = cells.shape
    wide = 4 * feat
    snaps, verts = steps, x_out.shape[0]
    chips = snaps // 2
    own = feat // snaps
    slots = tiles.shape[0]
    reach = slots // 2
    width = wide // COL_BLOCKS
    me, mv = lax.axis_index("snap"), lax.axis_index("vert")
    chip, core = me // 2, me % 2
    mate = 2 * chip + 1 - core

    loads = [
        pltpu.make_async_copy(src, dst, load_sem.at[n])
        for n, (src, dst) in enumerate([
            (input_any, input_w), (conv_out_any, conv_out), (tiles_any, tiles),
            (feats_any, feats), (conv_w_any, conv_w),
        ])
    ]
    for load in loads:
        load.start()

    barrier = pltpu.get_barrier_semaphore()
    for s in range(snaps):
        @pl.when(s != me)
        def _():
            pl.semaphore_signal(barrier, inc=1, device_id=(s, mv), device_id_type=MESH)
    for v in range(verts):
        @pl.when(v != mv)
        def _():
            pl.semaphore_signal(barrier, inc=1, device_id=(me, v), device_id_type=MESH)

    for k in range(4):
        cols = slice(k * feat, (k + 1) * feat)
        split_store(recur[:, cols].T, r_hi.at[cols, :], r_lo.at[cols, :])
    loads[0].wait()
    for k in range(4):
        cols = slice(k * feat, (k + 1) * feat)
        split_store(input_w[:, cols].T, i_hi.at[cols, :], i_lo.at[cols, :])
    rec[...] = jnp.zeros_like(rec)
    cell_grad[...] = jnp.zeros_like(cell_grad)
    pl.semaphore_wait(barrier, snaps + verts - 2)

    def step(t):
        before = jnp.maximum(t - 1, 0)
        live = (t > 0).astype(F32)
        part = lambda k: gates[t, :, k * feat : (k + 1) * feat].astype(F32)
        in_gate, forget, candidate, out_gate = part(0), part(1), part(2), part(3)
        squashed = jnp.tanh(cells[t].astype(F32))
        cell_before = cells[before].astype(F32) * live
        hidden = gates[before, :, 3 * feat :].astype(F32) * jnp.tanh(cell_before)
        hid_hi[t], hid_lo[t] = halves(hidden)
        total = grads[t] + rec[...]
        cell_total = cell_grad[...] + total * (out_gate * (1.0 - squashed * squashed))
        pieces = [
            cell_total * (candidate * in_gate * (1.0 - in_gate)),
            cell_total * (cell_before * forget * (1.0 - forget)),
            cell_total * (in_gate * (1.0 - candidate * candidate)),
            total * (squashed * out_gate * (1.0 - out_gate)),
        ]
        cell_grad[...] = cell_total * forget
        acc = None
        for k, piece in enumerate(pieces):
            cols = slice(k * feat, (k + 1) * feat)
            high, low = halves(piece)
            pre_hi[t, :, cols] = high
            pre_lo[t, :, cols] = low
            both = jnp.concatenate([high, low], axis=0)
            main = jnp.dot(both, r_hi[cols, :], preferred_element_type=F32)
            side = jnp.dot(high, r_lo[cols, :], preferred_element_type=F32)
            term = main[:rows] + (main[rows:] + side)
            acc = term if acc is None else acc + term
        rec[...] = acc

    def give(t):
        return remote(rounded.at[t], arrived.at[me], a_send.at[t], a_recv.at[me], (t, mv))

    def group(n, carry):
        base = steps - GROUP * (n + 1)

        def inner(j, c):
            step(base + GROUP - 1 - j)
            return c

        lax.fori_loop(0, GROUP, inner, 0)
        shape = (GROUP * rows, wide)
        value = dot3(
            pre_hi[pl.ds(base, GROUP)].reshape(shape), pre_lo[pl.ds(base, GROUP)].reshape(shape),
            i_hi[...], i_lo[...], ((1,), (0,)),
        )
        rounded[pl.ds(base, GROUP)] = value.astype(BF16).reshape(GROUP, rows, feat)
        for j in range(GROUP):
            t = base + j

            @pl.when(t != me)
            def _():
                give(t).start()
        return carry

    lax.fori_loop(0, steps // GROUP, group, 0)
    arrived[me] = rounded[me]

    loads[1].wait()
    flat = lambda ref: ref[...].reshape(steps * rows, feat)
    split_store(flat(conv_out), c_hi, c_lo)
    first = ((0,), (0,))

    def pair_copy(n):
        return remote(pair_out.at[n], pair_in.at[n], p_send.at[n], p_recv.at[n], (mate, mv))

    def along_z(n, q):
        return remote(
            z_out.at[n, q], z_in.at[n, chip], z_send.at[n, q], z_recv.at[n, chip], (2 * q + core, mv)
        )

    def from_z(n, q):
        return remote(
            z_out.at[n, q], z_in.at[n, q], z_send.at[n, q], z_recv.at[n, q], (2 * q + core, mv)
        )

    def make_terms(n):
        cols = slice(n * width, (n + 1) * width)
        p_hi = pre_hi[:, :, cols].reshape(steps * rows, width)
        p_lo = pre_lo[:, :, cols].reshape(steps * rows, width)
        value = dot3(c_hi[...], c_lo[...], p_hi, p_lo, first)
        terms[n, :, 0:own, :] = value.reshape(snaps, own, width)
        value = dot3(flat(hid_hi), flat(hid_lo), p_hi, p_lo, first)
        terms[n, :, own : 2 * own, :] = value.reshape(snaps, own, width)
        for q in range(chips):
            pair_out[n, q] = terms[n, 2 * q + 1 - core].astype(BF16)
        pair_copy(n).start()

    def chip_sum(n, q):
        return terms[n, 2 * q + core] + pair_in[n, q].astype(F32)

    def send_z(n):
        pair_copy(n).wait_recv()
        for q in range(chips):
            z_out[n, q] = chip_sum(n, q).astype(BF16)
        for q in range(chips):
            @pl.when(q != chip)
            def _():
                along_z(n, q).start()

    for n in range(COL_BLOCKS):
        make_terms(n)
        if n > 0:
            send_z(n - 1)

    for s in range(snaps):
        @pl.when(s != me)
        def _():
            remote(rounded.at[s], arrived.at[s], a_send.at[s], a_recv.at[s], (s, mv)).wait_recv()
    loads[2].wait()
    block = steps * rows
    mine = arrived[...].reshape(block, feat)

    def partial_copy(slot):
        return remote(
            away.at[slot], got.at[slot], t_send.at[slot], t_recv.at[slot], (me, mv + slot - reach)
        )

    def has_target(slot):
        return (mv + (slot - reach) >= 0) & (mv + (slot - reach) < verts)

    def has_source(slot):
        return (mv - (slot - reach) >= 0) & (mv - (slot - reach) < verts)

    ordered = [s for d in range(reach, 0, -1) for s in (reach - d, reach + d)]
    for slot in ordered + [reach]:
        value = lax.dot_general(
            tiles[slot], mine, (first, ((), ())), preferred_element_type=F32
        ) * present[slot].astype(F32)
        if slot == reach:
            z_grad[...] = value
        else:
            away[slot] = value.astype(BF16)

            @pl.when(has_target(slot))
            def _():
                partial_copy(slot).start()
            if slot == ordered[0]:
                send_z(COL_BLOCKS - 1)

    loads[3].wait()
    loads[4].wait()
    split_store(feats[...], n_hi, n_lo)
    split_store(conv_w[...], w_hi, w_lo)
    for slot in ordered[::-1]:
        @pl.when(has_source(slot))
        def _():
            partial_copy(slot).wait_recv()
            z_grad[...] += got[slot].astype(F32)
    split_store(z_grad[...], z_hi, z_lo)

    ct[...] = dot3(n_hi[...], n_lo[...], z_hi[...], z_lo[...], first).reshape(snaps, own, feat)
    for q in range(chips):
        cp_out[q] = ct[2 * q + 1 - core]
    conv_pair = remote(cp_out, cp_in, cp_send, cp_recv, (mate, mv))
    conv_pair.start()

    def conv_z(q, landing):
        return remote(
            cz_out.at[q], cz_in.at[landing], cz_send.at[q], cz_recv.at[landing], (2 * q + core, mv)
        )

    feat_out[...] = dot3(z_hi[...], z_lo[...], w_hi[...], w_lo[...], ((1,), (1,)))
    conv_pair.wait_recv()
    for q in range(chips):
        cz_out[q] = ct[2 * q + core] + cp_in[q]
    for q in range(chips):
        @pl.when(q != chip)
        def _():
            conv_z(q, chip).start()

    x_out[...] = jnp.zeros_like(x_out)
    for n in range(COL_BLOCKS):
        cols = slice(n * width, (n + 1) * width)
        full[:, cols] = chip_sum(n, chip)
        for q in range(chips):
            @pl.when(q != chip)
            def _():
                from_z(n, q).wait_recv()
                full[:, cols] += z_in[n, q].astype(F32)
    half = wide // 2
    share = 2 * own // verts
    for v in range(verts):
        for g in range(2):
            for j in range(share):
                h = share * v + j
                row = g * own + h // 2
                col = (h % 2) * half
                x_out[v, g * share + j : g * share + j + 1, :] = full[row : row + 1, col : col + half]

    def along_v(v, landing):
        return remote(x_out.at[v], x_in.at[landing], x_send.at[v], x_recv.at[landing], (me, v))

    for v in range(verts):
        @pl.when(v != mv)
        def _():
            along_v(v, mv).start()

    cx_out[...] = jnp.zeros_like(cx_out)
    cz_in[chip] = cz_out[chip]
    for q in range(chips):
        @pl.when(q != chip)
        def _():
            conv_z(q, q).wait_recv()
    summed = cz_in[0]
    for q in range(1, chips):
        summed += cz_in[q]
    pairs = verts // 2
    for j in range(pairs):
        cx_out[j, 0:share, :] = summed[share * j : share * (j + 1), :]

    def conv_v(v, landing):
        return remote(cx_out.at[v // 2], cx_in.at[landing], cx_send.at[v], cx_recv.at[landing], (me, v))

    for v in range(verts):
        @pl.when(v != mv)
        def _():
            conv_v(v, mv).start()
    x_in[mv] = x_out[mv]
    cx_in[mv] = cx_out[mv // 2]
    for v in range(verts):
        @pl.when(v != mv)
        def _():
            along_v(v, v).wait_recv()
    lstm_sum[...] = jnp.sum(x_in[...], axis=0)
    for v in range(verts):
        @pl.when(v != mv)
        def _():
            conv_v(v, v).wait_recv()
    conv_out_sum[...] = jnp.sum(cx_in[...], axis=0)

    for s in range(snaps):
        @pl.when(s != me)
        def _():
            give(s).wait_send()
    for n in range(COL_BLOCKS):
        pair_copy(n).wait_send()
        for q in range(chips):
            @pl.when(q != chip)
            def _():
                along_z(n, q).wait_send()
    for slot in ordered:
        @pl.when(has_target(slot))
        def _():
            partial_copy(slot).wait_send()
    conv_pair.wait_send()
    for q in range(chips):
        @pl.when(q != chip)
        def _():
            conv_z(q, chip).wait_send()
    for v in range(verts):
        @pl.when(v != mv)
        def _():
            along_v(v, mv).wait_send()
            conv_v(v, mv).wait_send()


def run_whole(
    present, gates, cells, grads, recur, input_w, conv_out, tiles, feats, conv_w, snaps, verts
):
    steps, rows, feat = cells.shape
    wide = 4 * feat
    slots, block, _ = tiles.shape
    chips, own, width = snaps // 2, feat // snaps, wide // COL_BLOCKS
    share = 2 * own // verts
    total = steps * rows
    vm = pl.BlockSpec(memory_space=pltpu.VMEM)
    hbm = pl.BlockSpec(memory_space=pl.ANY)
    b = lambda *s: pltpu.VMEM(s, BF16)
    f = lambda *s: pltpu.VMEM(s, F32)
    sem = lambda *s: pltpu.SemaphoreType.DMA(s)
    like = lambda a: pltpu.VMEM(a.shape, a.dtype)
    conv_rows = -(-share // 8) * 8
    lstm_rows = -(-2 * share // 8) * 8
    return pl.pallas_call(
        whole_kernel,
        in_specs=[pl.BlockSpec(memory_space=pltpu.SMEM)] + [vm] * 4 + [hbm] * 5,
        out_specs=[vm] * 3,
        out_shape=[
            jax.ShapeDtypeStruct((block, feat), F32),
            jax.ShapeDtypeStruct((conv_rows, feat), F32),
            jax.ShapeDtypeStruct((lstm_rows, wide // 2), F32),
        ],
        scratch_shapes=[
            like(input_w), like(conv_out), like(tiles), like(feats), like(conv_w),
            b(wide, feat), b(wide, feat), b(wide, feat), b(wide, feat), f(rows, feat), f(rows, feat),
            b(steps, rows, wide), b(steps, rows, wide), b(steps, rows, feat), b(steps, rows, feat),
            b(total, feat), b(total, feat), b(steps, rows, feat), b(steps, rows, feat),
            f(COL_BLOCKS, snaps, 2 * own, width),
            b(COL_BLOCKS, chips, 2 * own, width), b(COL_BLOCKS, chips, 2 * own, width),
            b(COL_BLOCKS, chips, 2 * own, width), b(COL_BLOCKS, chips, 2 * own, width),
            f(2 * own, wide), f(verts, lstm_rows, wide // 2), f(verts, lstm_rows, wide // 2),
            b(slots, block, feat), b(slots, block, feat), f(block, feat), b(block, feat), b(block, feat),
            b(feat, feat), b(feat, feat), b(block, feat), b(block, feat),
            f(snaps, own, feat), f(chips, own, feat), f(chips, own, feat),
            f(chips, own, feat), f(chips, own, feat),
            f(verts // 2, conv_rows, feat), f(verts, conv_rows, feat),
            sem(5), sem(snaps), sem(snaps), sem(COL_BLOCKS), sem(COL_BLOCKS),
            sem(COL_BLOCKS, chips), sem(COL_BLOCKS, chips), sem(verts), sem(verts),
            sem(slots), sem(slots), pltpu.SemaphoreType.DMA, pltpu.SemaphoreType.DMA,
            sem(chips), sem(chips), sem(verts), sem(verts),
        ],
        compiler_params=pltpu.CompilerParams(
            vmem_limit_bytes=VMEM_CAP, collective_id=0, has_side_effects=True
        ),
        name="whole",
    )(present, gates, cells, grads, recur, input_w, conv_out, tiles, feats, conv_w)


def local(
    saved_gates, saved_cells, conv_out, out_grad, input_weight, recur_weight,
    conv_weight, node_feats, tile_values, tile_mask,
):
    feat = saved_cells.shape[-1]
    snaps, verts = lax.axis_size("snap"), lax.axis_size("vert")
    slot_count = tile_values.shape[2]
    reach = slot_count // 2
    mv = lax.axis_index("vert")
    target = mv + jnp.arange(slot_count, dtype=jnp.int32) - reach
    inside = (target >= 0) & (target < verts)
    present = ((tile_mask[0, 0] == 1) & inside).astype(jnp.int32)
    feat_grad, conv, lstm = run_whole(
        present, saved_gates, saved_cells, out_grad, recur_weight, input_weight, conv_out,
        tile_values[0, 0], node_feats[0], conv_weight, snaps, verts,
    )
    share = 2 * (feat // snaps) // verts
    size = share * feat // 2
    conv = lax.dynamic_slice_in_dim(conv[:share].reshape(-1), (mv % 2) * size, size)
    return (
        feat_grad[None],
        conv,
        lstm[:share].reshape(-1),
        lstm[share : 2 * share].reshape(-1),
    )


def solution(mesh):
    along = P(None, ("vert", "snap"), None)
    placed = (
        along, along, along, along, P(), P(), P(),
        P("snap", "vert", None), P("snap", "vert", None, None, None), P("snap", "vert", None),
    )
    both = P(("snap", "vert"))
    return jax.shard_map(
        local,
        mesh=mesh,
        in_specs=placed,
        out_specs=(P("snap", "vert", None), both, both, both),
        check_vma=False,
    )
```

```python
import jax
import jax.numpy as jnp
from jax import lax
from jax.experimental import pallas as pl
from jax.experimental.pallas import tpu as pltpu
from jax.sharding import PartitionSpec as P

F32, BF16 = jnp.float32, jnp.bfloat16
VMEM_CAP = 62 * 1024 * 1024
COL_BLOCKS = 3
GROUP = 4
MESH = pl.DeviceIdType.MESH


def halves(value):
    high = value.astype(BF16)
    return high, (value - high.astype(F32)).astype(BF16)


def split_store(value, hi_ref, lo_ref):
    hi_ref[...], lo_ref[...] = halves(value)


def dot3(a_hi, a_lo, b_hi, b_lo, dims):
    one = lambda a, b: lax.dot_general(a, b, (dims, ((), ())), preferred_element_type=F32)
    return one(a_hi, b_hi) + (one(a_lo, b_hi) + one(a_hi, b_lo))


def remote(src, dst, send, recv, device):
    return pltpu.make_async_remote_copy(
        src_ref=src, dst_ref=dst, send_sem=send, recv_sem=recv, device_id=device, device_id_type=MESH
    )


def whole_kernel(
    mask, gates, cells, grads, recur, input_any, conv_out_any, tiles_any, feats_any, conv_w_any,
    feat_out, sums_out,
    input_w, conv_out, tiles, feats, conv_w,
    r_hi, r_lo, i_hi, i_lo, rec, cell_grad,
    pre_hi, pre_lo, hid_hi, hid_lo, c_hi, c_lo, rounded, arrived,
    terms, pair_out, pair_in, z_out, z_in, full, x_out, x_in,
    via_out, via_in, next_to, away, got, z_grad, z_hi, z_lo, w_hi, w_lo, n_hi, n_lo,
    ct, cp_out, cp_in, cz_out, cz_in, cx_out, cx_in,
    load_sem, a_send, a_recv, p_send, p_recv, z_send, z_recv, x_send, x_recv,
    v_send, v_recv, t_send, t_recv, cp_send, cp_recv, cz_send, cz_recv, cx_send, cx_recv,
):
    steps, rows, feat = cells.shape
    wide = 4 * feat
    snaps, verts = steps, x_out.shape[0]
    chips = snaps // 2
    own = feat // snaps
    slots = tiles.shape[0]
    reach = slots // 2
    width = wide // COL_BLOCKS
    me, mv = lax.axis_index("snap"), lax.axis_index("vert")
    chip, core = me // 2, me % 2
    mate = 2 * chip + 1 - core

    loads = [
        pltpu.make_async_copy(src, dst, load_sem.at[n])
        for n, (src, dst) in enumerate([
            (input_any, input_w), (conv_out_any, conv_out), (tiles_any, tiles),
            (feats_any, feats), (conv_w_any, conv_w),
        ])
    ]
    for load in loads:
        load.start()

    barrier = pltpu.get_barrier_semaphore()
    for s in range(snaps):
        @pl.when(s != me)
        def _():
            pl.semaphore_signal(barrier, inc=1, device_id=(s, mv), device_id_type=MESH)
    for v in range(verts):
        @pl.when(v != mv)
        def _():
            pl.semaphore_signal(barrier, inc=1, device_id=(me, v), device_id_type=MESH)

    for k in range(4):
        cols = slice(k * feat, (k + 1) * feat)
        split_store(recur[:, cols].T, r_hi.at[cols, :], r_lo.at[cols, :])
    loads[0].wait()
    for k in range(4):
        cols = slice(k * feat, (k + 1) * feat)
        split_store(input_w[:, cols].T, i_hi.at[cols, :], i_lo.at[cols, :])
    rec[...] = jnp.zeros_like(rec)
    cell_grad[...] = jnp.zeros_like(cell_grad)
    pl.semaphore_wait(barrier, snaps + verts - 2)

    def step(t):
        before = jnp.maximum(t - 1, 0)
        live = (t > 0).astype(F32)
        part = lambda k: gates[t, :, k * feat : (k + 1) * feat].astype(F32)
        in_gate, forget, candidate, out_gate = part(0), part(1), part(2), part(3)
        squashed = jnp.tanh(cells[t].astype(F32))
        cell_before = cells[before].astype(F32) * live
        hidden = gates[before, :, 3 * feat :].astype(F32) * jnp.tanh(cell_before)
        hid_hi[t], hid_lo[t] = halves(hidden)
        total = grads[t] + rec[...]
        cell_total = cell_grad[...] + total * (out_gate * (1.0 - squashed * squashed))
        pieces = [
            cell_total * (candidate * in_gate * (1.0 - in_gate)),
            cell_total * (cell_before * forget * (1.0 - forget)),
            cell_total * (in_gate * (1.0 - candidate * candidate)),
            total * (squashed * out_gate * (1.0 - out_gate)),
        ]
        cell_grad[...] = cell_total * forget
        acc = None
        for k, piece in enumerate(pieces):
            cols = slice(k * feat, (k + 1) * feat)
            high, low = halves(piece)
            pre_hi[t, :, cols] = high
            pre_lo[t, :, cols] = low
            both = jnp.concatenate([high, low], axis=0)
            main = jnp.dot(both, r_hi[cols, :], preferred_element_type=F32)
            side = jnp.dot(high, r_lo[cols, :], preferred_element_type=F32)
            term = main[:rows] + (main[rows:] + side)
            acc = term if acc is None else acc + term
        rec[...] = acc

    def give(t):
        return remote(rounded.at[t], arrived.at[me], a_send.at[t], a_recv.at[me], (t, mv))

    def group(base, size):
        def inner(j, c):
            step(base + size - 1 - j)
            return c

        lax.fori_loop(0, size, inner, 0)
        shape = (size * rows, wide)
        value = dot3(
            pre_hi[pl.ds(base, size)].reshape(shape), pre_lo[pl.ds(base, size)].reshape(shape),
            i_hi[...], i_lo[...], ((1,), (0,)),
        )
        rounded[pl.ds(base, size)] = value.astype(BF16).reshape(size, rows, feat)
        for j in range(size):
            t = base + j

            @pl.when(t != me)
            def _():
                give(t).start()

    def full_group(n, carry):
        group(steps - GROUP * (n + 1), GROUP)
        return carry

    lax.fori_loop(0, steps // GROUP - 1, full_group, 0)
    group(GROUP // 2, GROUP // 2)
    group(0, GROUP // 2)
    arrived[me] = rounded[me]

    loads[1].wait()
    flat = lambda ref: ref[...].reshape(steps * rows, feat)
    split_store(flat(conv_out), c_hi, c_lo)
    first = ((0,), (0,))

    def pair_copy(n):
        return remote(pair_out.at[n], pair_in.at[n], p_send.at[n], p_recv.at[n], (mate, mv))

    def along_z(n, q):
        return remote(
            z_out.at[n, q], z_in.at[n, chip], z_send.at[n, q], z_recv.at[n, chip], (2 * q + core, mv)
        )

    def from_z(n, q):
        return remote(
            z_out.at[n, q], z_in.at[n, q], z_send.at[n, q], z_recv.at[n, q], (2 * q + core, mv)
        )

    def make_terms(n):
        cols = slice(n * width, (n + 1) * width)
        p_hi = pre_hi[:, :, cols].reshape(steps * rows, width)
        p_lo = pre_lo[:, :, cols].reshape(steps * rows, width)
        value = dot3(c_hi[...], c_lo[...], p_hi, p_lo, first)
        terms[n, :, 0:own, :] = value.reshape(snaps, own, width)
        value = dot3(flat(hid_hi), flat(hid_lo), p_hi, p_lo, first)
        terms[n, :, own : 2 * own, :] = value.reshape(snaps, own, width)
        for q in range(chips):
            pair_out[n, q] = terms[n, 2 * q + 1 - core].astype(BF16)
        pair_copy(n).start()

    def chip_sum(n, q):
        return terms[n, 2 * q + core] + pair_in[n, q].astype(F32)

    def send_z(n):
        pair_copy(n).wait_recv()
        for q in range(chips):
            z_out[n, q] = chip_sum(n, q).astype(BF16)
        for q in range(chips):
            @pl.when(q != chip)
            def _():
                along_z(n, q).start()

    make_terms(0)

    for s in range(snaps):
        @pl.when(s != me)
        def _():
            remote(rounded.at[s], arrived.at[s], a_send.at[s], a_recv.at[s], (s, mv)).wait_recv()
    loads[2].wait()
    block = steps * rows
    mine = arrived[...].reshape(block, feat)

    parts_of = 2
    chunk = block // parts_of

    def near(d):
        return (mv + d >= 0) & (mv + d < verts)

    def via_copy(d, k):
        at = pl.ds(k * chunk, chunk)
        w = (d + 1) // 2
        return remote(
            via_out.at[w, at], via_in.at[w, at], v_send.at[w, k], v_recv.at[w, k], (me, mv + d)
        )

    def sum_copy(d, k):
        at = pl.ds(k * chunk, chunk)
        w = (d + 1) // 2
        return remote(away.at[w, at], got.at[w, at], t_send.at[w, k], t_recv.at[w, k], (me, mv + d))

    def product(slot):
        return lax.dot_general(
            tiles[slot], mine, (first, ((), ())), preferred_element_type=F32
        ) * (mask[0, 0, slot] == 1).astype(F32)

    for d in (1, -1):
        via_out[(d + 1) // 2] = product(reach + 2 * d).astype(BF16)

        @pl.when(near(2 * d))
        def _():
            for k in range(parts_of):
                via_copy(d, k).start()
    send_z(0)
    for d in (1, -1):
        next_to[(d + 1) // 2] = product(reach + d)

    def pass_on(k):
        at = pl.ds(k * chunk, chunk)
        for d in (1, -1):
            w = (d + 1) // 2

            @pl.when(near(d) & near(-d))
            def _():
                via_copy(d, k).wait_recv()
                away[w, at] = (next_to[w, at] + via_in[w, at].astype(F32)).astype(BF16)

            @pl.when(near(d) & jnp.logical_not(near(-d)))
            def _():
                away[w, at] = next_to[w, at].astype(BF16)

            @pl.when(near(d))
            def _():
                sum_copy(d, k).start()

    make_terms(1)
    pass_on(0)
    for n in range(2, COL_BLOCKS):
        send_z(n - 1)
        make_terms(n)
    pass_on(1)
    send_z(COL_BLOCKS - 1)
    z_grad[...] = product(reach)

    loads[3].wait()
    loads[4].wait()
    split_store(feats[...], n_hi, n_lo)
    split_store(conv_w[...], w_hi, w_lo)
    for k in range(parts_of):
        at = pl.ds(k * chunk, chunk)
        for d in (1, -1):
            @pl.when(near(-d))
            def _():
                sum_copy(d, k).wait_recv()
                z_grad[at] += got[(d + 1) // 2, at].astype(F32)
    split_store(z_grad[...], z_hi, z_lo)

    ct[...] = dot3(n_hi[...], n_lo[...], z_hi[...], z_lo[...], first).reshape(snaps, own, feat)
    for q in range(chips):
        cp_out[q] = ct[2 * q + 1 - core]
    conv_pair = remote(cp_out, cp_in, cp_send, cp_recv, (mate, mv))
    conv_pair.start()

    def conv_z(q, landing):
        return remote(
            cz_out.at[q], cz_in.at[landing], cz_send.at[q], cz_recv.at[landing], (2 * q + core, mv)
        )

    feat_out[...] = dot3(z_hi[...], z_lo[...], w_hi[...], w_lo[...], ((1,), (1,)))
    conv_pair.wait_recv()
    for q in range(chips):
        cz_out[q] = (ct[2 * q + core] + cp_in[q]).astype(BF16)
    for q in range(chips):
        @pl.when(q != chip)
        def _():
            conv_z(q, chip).start()

    x_out[...] = jnp.zeros_like(x_out)
    for n in range(COL_BLOCKS):
        cols = slice(n * width, (n + 1) * width)
        full[:, cols] = chip_sum(n, chip)
        for q in range(chips):
            @pl.when(q != chip)
            def _():
                from_z(n, q).wait_recv()
                full[:, cols] += z_in[n, q].astype(F32)
    half = wide // 2
    share = 2 * own // verts
    for v in range(verts):
        for g in range(2):
            for j in range(share):
                h = share * v + j
                row = g * own + h // 2
                col = (h % 2) * half
                x_out[v, g * share + j : g * share + j + 1, :] = full[row : row + 1, col : col + half]

    def along_v(v, landing):
        return remote(x_out.at[v], x_in.at[landing], x_send.at[v], x_recv.at[landing], (me, v))

    for v in range(verts):
        @pl.when(v != mv)
        def _():
            along_v(v, mv).start()

    cx_out[...] = jnp.zeros_like(cx_out)
    cz_in[chip] = cz_out[chip]
    for q in range(chips):
        @pl.when(q != chip)
        def _():
            conv_z(q, q).wait_recv()
    summed = cz_in[0].astype(F32)
    for q in range(1, chips):
        summed += cz_in[q].astype(F32)
    pairs = verts // 2
    for j in range(pairs):
        cx_out[j, 0:share, :] = summed[share * j : share * (j + 1), :]

    def conv_v(v, landing):
        return remote(cx_out.at[v // 2], cx_in.at[landing], cx_send.at[v], cx_recv.at[landing], (me, v))

    for v in range(verts):
        @pl.when(v != mv)
        def _():
            conv_v(v, mv).start()
    x_in[mv] = x_out[mv]
    cx_in[mv] = cx_out[mv // 2]
    for v in range(verts):
        @pl.when(v != mv)
        def _():
            along_v(v, v).wait_recv()
    summed = jnp.sum(x_in[...], axis=0)
    parts = half // 128
    for n in range(2 * share):
        for k in range(parts):
            at = n * parts + k
            sums_out[at : at + 1, :] = summed[n : n + 1, k * 128 : (k + 1) * 128]
    for v in range(verts):
        @pl.when(v != mv)
        def _():
            conv_v(v, v).wait_recv()
    summed = jnp.sum(cx_in[...], axis=0)
    flat_rows = [
        summed[n : n + 1, k * 128 : (k + 1) * 128] for n in range(share) for k in range(feat // 128)
    ]
    base, skip = 2 * share * parts, share * feat // 256
    shift = share * feat // 2 - skip * 128
    for n in range(skip + (1 if shift else 0)):
        late = flat_rows[skip + n]
        if shift and skip + n + 1 < len(flat_rows):
            late = jnp.concatenate([late[:, shift:], flat_rows[skip + n + 1][:, :shift]], axis=1)
        elif shift:
            late = jnp.concatenate([late[:, shift:], late[:, :shift]], axis=1)
        sums_out[base + n : base + n + 1, :] = jnp.where(mv % 2 == 0, flat_rows[n], late)

    for s in range(snaps):
        @pl.when(s != me)
        def _():
            give(s).wait_send()
    for n in range(COL_BLOCKS):
        pair_copy(n).wait_send()
        for q in range(chips):
            @pl.when(q != chip)
            def _():
                along_z(n, q).wait_send()
    for k in range(parts_of):
        for d in (1, -1):
            @pl.when(near(2 * d))
            def _():
                via_copy(d, k).wait_send()

            @pl.when(near(d))
            def _():
                sum_copy(d, k).wait_send()
    conv_pair.wait_send()
    for q in range(chips):
        @pl.when(q != chip)
        def _():
            conv_z(q, chip).wait_send()
    for v in range(verts):
        @pl.when(v != mv)
        def _():
            along_v(v, mv).wait_send()
            conv_v(v, mv).wait_send()


def run_whole(
    mask, gates, cells, grads, recur, input_w, conv_out, tiles, feats, conv_w, snaps, verts
):
    steps, rows, feat = cells.shape
    wide = 4 * feat
    slots, block, _ = tiles.shape
    chips, own, width = snaps // 2, feat // snaps, wide // COL_BLOCKS
    share = 2 * own // verts
    total = steps * rows
    vm = pl.BlockSpec(memory_space=pltpu.VMEM)
    hbm = pl.BlockSpec(memory_space=pl.ANY)
    b = lambda *s: pltpu.VMEM(s, BF16)
    f = lambda *s: pltpu.VMEM(s, F32)
    sem = lambda *s: pltpu.SemaphoreType.DMA(s)
    like = lambda a: pltpu.VMEM(a.shape, a.dtype)
    conv_rows = -(-share // 8) * 8
    lstm_rows = -(-2 * share // 8) * 8
    sum_rows = -(-(2 * share * wide // 256 + share * feat // 256 + 1) // 8) * 8
    return pl.pallas_call(
        whole_kernel,
        in_specs=[pl.BlockSpec(memory_space=pltpu.SMEM)] + [vm] * 4 + [hbm] * 5,
        out_specs=[vm] * 2,
        out_shape=[
            jax.ShapeDtypeStruct((block, feat), F32),
            jax.ShapeDtypeStruct((sum_rows, 128), F32),
        ],
        scratch_shapes=[
            like(input_w), like(conv_out), like(tiles), like(feats), like(conv_w),
            b(wide, feat), b(wide, feat), b(wide, feat), b(wide, feat), f(rows, feat), f(rows, feat),
            b(steps, rows, wide), b(steps, rows, wide), b(steps, rows, feat), b(steps, rows, feat),
            b(total, feat), b(total, feat), b(steps, rows, feat), b(steps, rows, feat),
            f(COL_BLOCKS, snaps, 2 * own, width),
            b(COL_BLOCKS, chips, 2 * own, width), b(COL_BLOCKS, chips, 2 * own, width),
            b(COL_BLOCKS, chips, 2 * own, width), b(COL_BLOCKS, chips, 2 * own, width),
            f(2 * own, wide), f(verts, lstm_rows, wide // 2), f(verts, lstm_rows, wide // 2),
            b(2, block, feat), b(2, block, feat), f(2, block, feat), b(2, block, feat),
            b(2, block, feat), f(block, feat), b(block, feat), b(block, feat),
            b(feat, feat), b(feat, feat), b(block, feat), b(block, feat),
            f(snaps, own, feat), f(chips, own, feat), f(chips, own, feat),
            b(chips, own, feat), b(chips, own, feat),
            f(verts // 2, conv_rows, feat), f(verts, conv_rows, feat),
            sem(5), sem(snaps), sem(snaps), sem(COL_BLOCKS), sem(COL_BLOCKS),
            sem(COL_BLOCKS, chips), sem(COL_BLOCKS, chips), sem(verts), sem(verts),
            sem(2, 2), sem(2, 2), sem(2, 2), sem(2, 2), pltpu.SemaphoreType.DMA, pltpu.SemaphoreType.DMA,
            sem(chips), sem(chips), sem(verts), sem(verts),
        ],
        compiler_params=pltpu.CompilerParams(
            vmem_limit_bytes=VMEM_CAP, collective_id=0, has_side_effects=True
        ),
        name="whole",
    )(mask, gates, cells, grads, recur, input_w, conv_out, tiles, feats, conv_w)


def local(
    saved_gates, saved_cells, conv_out, out_grad, input_weight, recur_weight,
    conv_weight, node_feats, tile_values, tile_mask,
):
    feat = saved_cells.shape[-1]
    snaps, verts = lax.axis_size("snap"), lax.axis_size("vert")
    feat_grad, sums = run_whole(
        tile_mask, saved_gates, saved_cells, out_grad, recur_weight, input_weight, conv_out,
        tile_values[0, 0], node_feats[0], conv_weight, snaps, verts,
    )
    share = 2 * (feat // snaps) // verts
    size = share * feat // 2
    flat = sums.reshape(-1)
    each = 4 * size
    return (feat_grad[None], flat[2 * each : 2 * each + size], flat[:each], flat[each : 2 * each])


def solution(mesh):
    along = P(None, ("vert", "snap"), None)
    placed = (
        along, along, along, along, P(), P(), P(),
        P("snap", "vert", None), P("snap", "vert", None, None, None), P("snap", "vert", None),
    )
    both = P(("snap", "vert"))
    return jax.shard_map(
        local,
        mesh=mesh,
        in_specs=placed,
        out_specs=(P("snap", "vert", None), both, both, both),
        check_vma=False,
    )
```

```python
import jax
import jax.numpy as jnp
from jax import lax
from jax.experimental import pallas as pl
from jax.experimental.pallas import tpu as pltpu
from jax.sharding import PartitionSpec as P

F32, BF16 = jnp.float32, jnp.bfloat16
VMEM_CAP = 62 * 1024 * 1024
COL_BLOCKS = 3
GROUP = 4
MESH = pl.DeviceIdType.MESH


def halves(value):
    high = value.astype(BF16)
    return high, (value - high.astype(F32)).astype(BF16)


def split_store(value, hi_ref, lo_ref):
    hi_ref[...], lo_ref[...] = halves(value)


def dot3(a_hi, a_lo, b_hi, b_lo, dims):
    one = lambda a, b: lax.dot_general(a, b, (dims, ((), ())), preferred_element_type=F32)
    return one(a_hi, b_hi) + (one(a_lo, b_hi) + one(a_hi, b_lo))


def remote(src, dst, send, recv, device):
    return pltpu.make_async_remote_copy(
        src_ref=src, dst_ref=dst, send_sem=send, recv_sem=recv, device_id=device, device_id_type=MESH
    )


def far_first(count):
    return sorted(range(1, count), key=lambda k: -min(k, count - k))


def whole_kernel(
    mask, gates, cells, grads, recur, input_any, conv_out_any, tiles_any, feats_any, conv_w_any,
    feat_out, sums_out,
    input_w, conv_out, tiles, feats, conv_w,
    r_hi, r_lo, i_hi, i_lo, rec, cell_grad,
    pre_hi, pre_lo, hid_hi, hid_lo, c_hi, c_lo, rounded, arrived,
    terms, pair_out, pair_in, z_out, z_in, full, x_out, x_in,
    via_out, via_in, next_to, away, got, z_grad, z_hi, z_lo, w_hi, w_lo, n_hi, n_lo,
    ct, cp_out, cp_in, cz_out, cz_in, cx_out, cx_in,
    load_sem, a_send, a_recv, p_send, p_recv, z_send, z_recv, x_send, x_recv,
    v_send, v_recv, t_send, t_recv, cp_send, cp_recv, cz_send, cz_recv, cx_send, cx_recv,
):
    steps, rows, feat = cells.shape
    wide = 4 * feat
    snaps, verts = steps, x_out.shape[0]
    chips = snaps // 2
    own = feat // snaps
    slots = tiles.shape[0]
    reach = slots // 2
    width = wide // COL_BLOCKS
    me, mv = lax.axis_index("snap"), lax.axis_index("vert")
    chip, core = me // 2, me % 2
    mate = 2 * chip + 1 - core

    loads = [
        pltpu.make_async_copy(src, dst, load_sem.at[n])
        for n, (src, dst) in enumerate([
            (input_any, input_w), (conv_out_any, conv_out), (tiles_any, tiles),
            (feats_any, feats), (conv_w_any, conv_w),
        ])
    ]
    for load in loads:
        load.start()

    barrier = pltpu.get_barrier_semaphore()
    for s in range(snaps):
        @pl.when(s != me)
        def _():
            pl.semaphore_signal(barrier, inc=1, device_id=(s, mv), device_id_type=MESH)
    for v in range(verts):
        @pl.when(v != mv)
        def _():
            pl.semaphore_signal(barrier, inc=1, device_id=(me, v), device_id_type=MESH)

    for k in range(4):
        cols = slice(k * feat, (k + 1) * feat)
        split_store(recur[:, cols].T, r_hi.at[cols, :], r_lo.at[cols, :])
    loads[0].wait()
    for k in range(4):
        cols = slice(k * feat, (k + 1) * feat)
        split_store(input_w[:, cols].T, i_hi.at[cols, :], i_lo.at[cols, :])
    rec[...] = jnp.zeros_like(rec)
    cell_grad[...] = jnp.zeros_like(cell_grad)
    pl.semaphore_wait(barrier, snaps + verts - 2)

    def step(t):
        before = jnp.maximum(t - 1, 0)
        live = (t > 0).astype(F32)
        part = lambda k: gates[t, :, k * feat : (k + 1) * feat].astype(F32)
        in_gate, forget, candidate, out_gate = part(0), part(1), part(2), part(3)
        squashed = jnp.tanh(cells[t].astype(F32))
        cell_before = cells[before].astype(F32) * live
        hidden = gates[before, :, 3 * feat :].astype(F32) * jnp.tanh(cell_before)
        hid_hi[t], hid_lo[t] = halves(hidden)
        total = grads[t] + rec[...]
        cell_total = cell_grad[...] + total * (out_gate * (1.0 - squashed * squashed))
        pieces = [
            cell_total * (candidate * in_gate * (1.0 - in_gate)),
            cell_total * (cell_before * forget * (1.0 - forget)),
            cell_total * (in_gate * (1.0 - candidate * candidate)),
            total * (squashed * out_gate * (1.0 - out_gate)),
        ]
        cell_grad[...] = cell_total * forget
        acc = None
        for k, piece in enumerate(pieces):
            cols = slice(k * feat, (k + 1) * feat)
            high, low = halves(piece)
            pre_hi[t, :, cols] = high
            pre_lo[t, :, cols] = low
            both = jnp.concatenate([high, low], axis=0)
            main = jnp.dot(both, r_hi[cols, :], preferred_element_type=F32)
            side = jnp.dot(high, r_lo[cols, :], preferred_element_type=F32)
            term = main[:rows] + (main[rows:] + side)
            acc = term if acc is None else acc + term
        rec[...] = acc

    def give(t):
        return remote(rounded.at[t], arrived.at[me], a_send.at[t], a_recv.at[me], (t, mv))

    def group(base, size):
        def inner(j, c):
            step(base + size - 1 - j)
            return c

        lax.fori_loop(0, size, inner, 0)
        shape = (size * rows, wide)
        value = dot3(
            pre_hi[pl.ds(base, size)].reshape(shape), pre_lo[pl.ds(base, size)].reshape(shape),
            i_hi[...], i_lo[...], ((1,), (0,)),
        )
        rounded[pl.ds(base, size)] = value.astype(BF16).reshape(size, rows, feat)
        for j in range(size):
            t = base + j

            @pl.when(t != me)
            def _():
                give(t).start()

    def full_group(n, carry):
        group(steps - GROUP * (n + 1), GROUP)
        return carry

    lax.fori_loop(0, steps // GROUP - 1, full_group, 0)
    group(GROUP // 2, GROUP // 2)
    group(0, GROUP // 2)
    arrived[me] = rounded[me]

    loads[1].wait()
    flat = lambda ref: ref[...].reshape(steps * rows, feat)
    split_store(flat(conv_out), c_hi, c_lo)
    first = ((0,), (0,))

    def pair_copy(n):
        return remote(pair_out.at[n], pair_in.at[n], p_send.at[n], p_recv.at[n], (mate, mv))

    def along_z(n, q):
        return remote(
            z_out.at[n, q], z_in.at[n, chip], z_send.at[n, q], z_recv.at[n, chip], (2 * q + core, mv)
        )

    def from_z(n, q):
        return remote(
            z_out.at[n, q], z_in.at[n, q], z_send.at[n, q], z_recv.at[n, q], (2 * q + core, mv)
        )

    def make_terms(n):
        cols = slice(n * width, (n + 1) * width)
        p_hi = pre_hi[:, :, cols].reshape(steps * rows, width)
        p_lo = pre_lo[:, :, cols].reshape(steps * rows, width)
        value = dot3(c_hi[...], c_lo[...], p_hi, p_lo, first)
        terms[n, :, 0:own, :] = value.reshape(snaps, own, width)
        value = dot3(flat(hid_hi), flat(hid_lo), p_hi, p_lo, first)
        terms[n, :, own : 2 * own, :] = value.reshape(snaps, own, width)
        for q in range(chips):
            pair_out[n, q] = terms[n, 2 * q + 1 - core].astype(BF16)
        pair_copy(n).start()

    def chip_sum(n, q):
        return terms[n, 2 * q + core] + pair_in[n, q].astype(F32)

    def send_z(n):
        pair_copy(n).wait_recv()
        for q in range(chips):
            z_out[n, q] = chip_sum(n, q).astype(BF16)
        for k in far_first(chips):
            along_z(n, lax.rem(chip + k, chips)).start()

    make_terms(0)

    for s in range(snaps):
        @pl.when(s != me)
        def _():
            remote(rounded.at[s], arrived.at[s], a_send.at[s], a_recv.at[s], (s, mv)).wait_recv()
    loads[2].wait()
    block = steps * rows
    mine = arrived[...].reshape(block, feat)

    parts_of = 2
    chunk = block // parts_of

    def near(d):
        return (mv + d >= 0) & (mv + d < verts)

    def via_copy(d, k):
        at = pl.ds(k * chunk, chunk)
        w = (d + 1) // 2
        return remote(
            via_out.at[w, at], via_in.at[w, at], v_send.at[w, k], v_recv.at[w, k], (me, mv + d)
        )

    def sum_copy(d, k):
        at = pl.ds(k * chunk, chunk)
        w = (d + 1) // 2
        return remote(away.at[w, at], got.at[w, at], t_send.at[w, k], t_recv.at[w, k], (me, mv + d))

    def product(slot):
        return lax.dot_general(
            tiles[slot], mine, (first, ((), ())), preferred_element_type=F32
        ) * (mask[0, 0, slot] == 1).astype(F32)

    for d in (1, -1):
        via_out[(d + 1) // 2] = product(reach + 2 * d).astype(BF16)

        @pl.when(near(2 * d))
        def _():
            for k in range(parts_of):
                via_copy(d, k).start()
    send_z(0)
    for d in (1, -1):
        next_to[(d + 1) // 2] = product(reach + d)

    def pass_on(k):
        at = pl.ds(k * chunk, chunk)
        for d in (1, -1):
            w = (d + 1) // 2

            @pl.when(near(d) & near(-d))
            def _():
                via_copy(d, k).wait_recv()
                away[w, at] = (next_to[w, at] + via_in[w, at].astype(F32)).astype(BF16)

            @pl.when(near(d) & jnp.logical_not(near(-d)))
            def _():
                away[w, at] = next_to[w, at].astype(BF16)

            @pl.when(near(d))
            def _():
                sum_copy(d, k).start()

    make_terms(1)
    pass_on(0)
    for n in range(2, COL_BLOCKS):
        send_z(n - 1)
        make_terms(n)
    pass_on(1)
    send_z(COL_BLOCKS - 1)
    z_grad[...] = product(reach)

    loads[3].wait()
    loads[4].wait()
    split_store(feats[...], n_hi, n_lo)
    split_store(conv_w[...], w_hi, w_lo)
    for k in range(parts_of):
        at = pl.ds(k * chunk, chunk)
        for d in (1, -1):
            @pl.when(near(-d))
            def _():
                sum_copy(d, k).wait_recv()
                z_grad[at] += got[(d + 1) // 2, at].astype(F32)
    split_store(z_grad[...], z_hi, z_lo)

    ct[...] = dot3(n_hi[...], n_lo[...], z_hi[...], z_lo[...], first).reshape(snaps, own, feat)
    for q in range(chips):
        cp_out[q] = ct[2 * q + 1 - core]
    conv_pair = remote(cp_out, cp_in, cp_send, cp_recv, (mate, mv))
    conv_pair.start()

    def conv_z(q, landing):
        return remote(
            cz_out.at[q], cz_in.at[landing], cz_send.at[q], cz_recv.at[landing], (2 * q + core, mv)
        )

    feat_out[...] = dot3(z_hi[...], z_lo[...], w_hi[...], w_lo[...], ((1,), (1,)))
    conv_pair.wait_recv()
    for q in range(chips):
        cz_out[q] = (ct[2 * q + core] + cp_in[q]).astype(BF16)
    for k in far_first(chips):
        conv_z(lax.rem(chip + k, chips), chip).start()

    x_out[...] = jnp.zeros_like(x_out)
    for n in range(COL_BLOCKS):
        cols = slice(n * width, (n + 1) * width)
        full[:, cols] = chip_sum(n, chip)
        for q in range(chips):
            @pl.when(q != chip)
            def _():
                from_z(n, q).wait_recv()
                full[:, cols] += z_in[n, q].astype(F32)
    half = wide // 2
    share = 2 * own // verts
    for v in range(verts):
        for g in range(2):
            for j in range(share):
                h = share * v + j
                row = g * own + h // 2
                col = (h % 2) * half
                x_out[v, g * share + j : g * share + j + 1, :] = full[row : row + 1, col : col + half]

    def along_v(v, landing):
        return remote(x_out.at[v], x_in.at[landing], x_send.at[v], x_recv.at[landing], (me, v))

    for k in range(1, verts):
        along_v(lax.rem(mv + k, verts), mv).start()

    cx_out[...] = jnp.zeros_like(cx_out)
    cz_in[chip] = cz_out[chip]
    for q in range(chips):
        @pl.when(q != chip)
        def _():
            conv_z(q, q).wait_recv()
    summed = cz_in[0].astype(F32)
    for q in range(1, chips):
        summed += cz_in[q].astype(F32)
    pairs = verts // 2
    for j in range(pairs):
        cx_out[j, 0:share, :] = summed[share * j : share * (j + 1), :]

    def conv_v(v, landing):
        return remote(cx_out.at[v // 2], cx_in.at[landing], cx_send.at[v], cx_recv.at[landing], (me, v))

    for k in range(1, verts):
        conv_v(lax.rem(mv + k, verts), mv).start()
    x_in[mv] = x_out[mv]
    cx_in[mv] = cx_out[mv // 2]
    for v in range(verts):
        @pl.when(v != mv)
        def _():
            along_v(v, v).wait_recv()
    summed = jnp.sum(x_in[...], axis=0)
    parts = half // 128
    for n in range(2 * share):
        for k in range(parts):
            at = n * parts + k
            sums_out[at : at + 1, :] = summed[n : n + 1, k * 128 : (k + 1) * 128]
    for v in range(verts):
        @pl.when(v != mv)
        def _():
            conv_v(v, v).wait_recv()
    summed = jnp.sum(cx_in[...], axis=0)
    flat_rows = [
        summed[n : n + 1, k * 128 : (k + 1) * 128] for n in range(share) for k in range(feat // 128)
    ]
    base, skip = 2 * share * parts, share * feat // 256
    shift = share * feat // 2 - skip * 128
    for n in range(skip + (1 if shift else 0)):
        late = flat_rows[skip + n]
        if shift and skip + n + 1 < len(flat_rows):
            late = jnp.concatenate([late[:, shift:], flat_rows[skip + n + 1][:, :shift]], axis=1)
        elif shift:
            late = jnp.concatenate([late[:, shift:], late[:, :shift]], axis=1)
        sums_out[base + n : base + n + 1, :] = jnp.where(mv % 2 == 0, flat_rows[n], late)

    for s in range(snaps):
        @pl.when(s != me)
        def _():
            give(s).wait_send()
    for n in range(COL_BLOCKS):
        pair_copy(n).wait_send()
        for q in range(chips):
            @pl.when(q != chip)
            def _():
                along_z(n, q).wait_send()
    for k in range(parts_of):
        for d in (1, -1):
            @pl.when(near(2 * d))
            def _():
                via_copy(d, k).wait_send()

            @pl.when(near(d))
            def _():
                sum_copy(d, k).wait_send()
    conv_pair.wait_send()
    for q in range(chips):
        @pl.when(q != chip)
        def _():
            conv_z(q, chip).wait_send()
    for v in range(verts):
        @pl.when(v != mv)
        def _():
            along_v(v, mv).wait_send()
            conv_v(v, mv).wait_send()


def run_whole(
    mask, gates, cells, grads, recur, input_w, conv_out, tiles, feats, conv_w, snaps, verts
):
    steps, rows, feat = cells.shape
    wide = 4 * feat
    slots, block, _ = tiles.shape
    chips, own, width = snaps // 2, feat // snaps, wide // COL_BLOCKS
    share = 2 * own // verts
    total = steps * rows
    vm = pl.BlockSpec(memory_space=pltpu.VMEM)
    hbm = pl.BlockSpec(memory_space=pl.ANY)
    b = lambda *s: pltpu.VMEM(s, BF16)
    f = lambda *s: pltpu.VMEM(s, F32)
    sem = lambda *s: pltpu.SemaphoreType.DMA(s)
    like = lambda a: pltpu.VMEM(a.shape, a.dtype)
    conv_rows = -(-share // 8) * 8
    lstm_rows = -(-2 * share // 8) * 8
    sum_rows = -(-(2 * share * wide // 256 + share * feat // 256 + 1) // 8) * 8
    return pl.pallas_call(
        whole_kernel,
        in_specs=[pl.BlockSpec(memory_space=pltpu.SMEM)] + [vm] * 4 + [hbm] * 5,
        out_specs=[vm] * 2,
        out_shape=[
            jax.ShapeDtypeStruct((block, feat), F32),
            jax.ShapeDtypeStruct((sum_rows, 128), F32),
        ],
        scratch_shapes=[
            like(input_w), like(conv_out), like(tiles), like(feats), like(conv_w),
            b(wide, feat), b(wide, feat), b(wide, feat), b(wide, feat), f(rows, feat), f(rows, feat),
            b(steps, rows, wide), b(steps, rows, wide), b(steps, rows, feat), b(steps, rows, feat),
            b(total, feat), b(total, feat), b(steps, rows, feat), b(steps, rows, feat),
            f(COL_BLOCKS, snaps, 2 * own, width),
            b(COL_BLOCKS, chips, 2 * own, width), b(COL_BLOCKS, chips, 2 * own, width),
            b(COL_BLOCKS, chips, 2 * own, width), b(COL_BLOCKS, chips, 2 * own, width),
            f(2 * own, wide), f(verts, lstm_rows, wide // 2), f(verts, lstm_rows, wide // 2),
            b(2, block, feat), b(2, block, feat), f(2, block, feat), b(2, block, feat),
            b(2, block, feat), f(block, feat), b(block, feat), b(block, feat),
            b(feat, feat), b(feat, feat), b(block, feat), b(block, feat),
            f(snaps, own, feat), f(chips, own, feat), f(chips, own, feat),
            b(chips, own, feat), b(chips, own, feat),
            f(verts // 2, conv_rows, feat), f(verts, conv_rows, feat),
            sem(5), sem(snaps), sem(snaps), sem(COL_BLOCKS), sem(COL_BLOCKS),
            sem(COL_BLOCKS, chips), sem(COL_BLOCKS, chips), sem(verts), sem(verts),
            sem(2, 2), sem(2, 2), sem(2, 2), sem(2, 2), pltpu.SemaphoreType.DMA, pltpu.SemaphoreType.DMA,
            sem(chips), sem(chips), sem(verts), sem(verts),
        ],
        compiler_params=pltpu.CompilerParams(
            vmem_limit_bytes=VMEM_CAP, collective_id=0, has_side_effects=True
        ),
        name="whole",
    )(mask, gates, cells, grads, recur, input_w, conv_out, tiles, feats, conv_w)


def local(
    saved_gates, saved_cells, conv_out, out_grad, input_weight, recur_weight,
    conv_weight, node_feats, tile_values, tile_mask,
):
    feat = saved_cells.shape[-1]
    snaps, verts = lax.axis_size("snap"), lax.axis_size("vert")
    feat_grad, sums = run_whole(
        tile_mask, saved_gates, saved_cells, out_grad, recur_weight, input_weight, conv_out,
        tile_values[0, 0], node_feats[0], conv_weight, snaps, verts,
    )
    share = 2 * (feat // snaps) // verts
    size = share * feat // 2
    flat = sums.reshape(-1)
    each = 4 * size
    return (feat_grad[None], flat[2 * each : 2 * each + size], flat[:each], flat[each : 2 * each])


def solution(mesh):
    along = P(None, ("vert", "snap"), None)
    placed = (
        along, along, along, along, P(), P(), P(),
        P("snap", "vert", None), P("snap", "vert", None, None, None), P("snap", "vert", None),
    )
    both = P(("snap", "vert"))
    return jax.shard_map(
        local,
        mesh=mesh,
        in_specs=placed,
        out_specs=(P("snap", "vert", None), both, both, both),
        check_vma=False,
    )
```
